32 devices in a mesh: fsdp: 8 (over z, y), dp: 4 (over x, core).
Axes of the slice: x: 2, y: 2, z: 4, core: 2. Of those that a mesh axis runs over, the one named last changes fastest.
Arguments:
- tokens: bfloat16 [192, 196, 512], P(('fsdp', 'dp')), may hold values from -6 to 6
- out_grad: bfloat16 [192, 196, 512], P(('fsdp', 'dp')), may hold values from -6 to 6
- image_counts: int32 [32], P(('fsdp', 'dp')), may hold values from 1 to 6, as said below
- table_index: int32 [49, 49], replicated, may hold values from 0 to 168, as said below
- bias_table: float32 [169, 16], replicated, may hold values from -210 to 210
- w_input: bfloat16 [512, 1536], P(('fsdp', 'dp')), may hold values from -3 to 3
- bias_query: bfloat16 [512], P(('fsdp', 'dp')), may hold values from -3 to 3
- bias_value: bfloat16 [512], P(('fsdp', 'dp')), may hold values from -3 to 3
- w_output: bfloat16 [512, 512], P(('fsdp', 'dp')), may hold values from -0.75 to 0.75
- bias_output: bfloat16 [512], P(('fsdp', 'dp')), may hold values from -3 to 3
- w_up: bfloat16 [512, 2048], P(('fsdp', 'dp')), may hold values from -0.25 to 0.25
- bias_up: bfloat16 [2048], P(('fsdp', 'dp')), may hold values from -3 to 3
- w_down: bfloat16 [2048, 512], P(('fsdp', 'dp')), may hold values from -0.1875 to 0.1875
- bias_down: bfloat16 [512], P(('fsdp', 'dp')), may hold values from -3 to 3
- first_gain: bfloat16 [512], P(('fsdp', 'dp')), may hold values from 0.5 to 1.5
- first_shift: bfloat16 [512], P(('fsdp', 'dp')), may hold values from -2 to 2
- second_gain: bfloat16 [512], P(('fsdp', 'dp')), may hold values from 0.5 to 1.5
- second_shift: bfloat16 [512], P(('fsdp', 'dp')), may hold values from -2 to 2
Outputs:
- mixed: bfloat16 [192, 196, 512], P(('fsdp', 'dp'))
- grad_tokens: float32 [192, 196, 512], P(('fsdp', 'dp'))
- grad_w_input: float32 [512, 1536], P(('fsdp', 'dp'))
- grad_bias_query: float32 [512], P(('fsdp', 'dp'))
- grad_bias_value: float32 [512], P(('fsdp', 'dp'))
- grad_w_output: float32 [512, 512], P(('fsdp', 'dp'))
- grad_bias_output: float32 [512], P(('fsdp', 'dp'))
- grad_w_up: float32 [512, 2048], P(('fsdp', 'dp'))
- grad_bias_up: float32 [2048], P(('fsdp', 'dp'))
- grad_w_down: float32 [2048, 512], P(('fsdp', 'dp'))
- grad_bias_down: float32 [512], P(('fsdp', 'dp'))
- grad_first_gain: float32 [512], P(('fsdp', 'dp'))
- grad_first_shift: float32 [512], P(('fsdp', 'dp'))
- grad_second_gain: float32 [512], P(('fsdp', 'dp'))
- grad_second_shift: float32 [512], P(('fsdp', 'dp'))
- grad_table: float32 [169, 16], replicated
The draws below stay inside these ranges and needn't reach their ends.
Inputs may be any that keep to these rules, and one draw needn't show every extreme that they name: `image_counts`: at least one device holds 6 live images; a device's live images fill its first slots. table_index[i, j] depends only on the offset between positions i and j of the 7 x 7 window, and distinct offsets have distinct entries.
All inputs are finite; a program needn't handle non-finite values.
Results may differ from the reference program's by a relative error of at most 0.0075.
The reference program's roundings to bfloat16 on the way count: a program that leaves them out, or rounds other values in their place, can miss the bound.
Values may be sent and summed in bfloat16 or wider, within the bound.
A program may use at most 192 MiB of HBM per device.

```python
import jax
import jax.numpy as jnp
from jax import lax

D = 512
HEADS = 16
HDIM = 32
HID = 2048
SIDE = 7
IMG_DEV = 6
WIN = 49
TOK_IMG = 196
NREL = 169
HOLDERS = 32
IMAGES = 192


def draw_image_counts(key, part):
    base = jax.random.randint(jax.random.fold_in(key, 1), (HOLDERS,), 1, IMG_DEV + 1)
    chosen = jax.random.randint(jax.random.fold_in(key, 2), (), 0, HOLDERS)
    return jnp.where(jnp.arange(HOLDERS) == chosen, IMG_DEV, base).astype(jnp.int32)


def draw_table_index(key, part):
    order = jax.random.permutation(jax.random.fold_in(key, 3), NREL).astype(jnp.int32)
    cells = jnp.arange(WIN, dtype=jnp.int32)
    row_pos = cells // SIDE
    col_pos = cells % SIDE
    offset = (row_pos[:, None] - row_pos[None, :] + SIDE - 1) * (2 * SIDE - 1) + (col_pos[:, None] - col_pos[None, :] + SIDE - 1)
    return order[offset].astype(jnp.int32)


def draw_bias_table(key, part):
    return jnp.clip(jax.random.normal(jax.random.fold_in(key, 5), (NREL, HEADS), jnp.float32), -4.0, 4.0)


def draw_w_input(key, part):
    entries = jnp.clip(jax.random.normal(key, (D, 3 * D), jnp.float32), -4.0, 4.0)
    return (entries * D ** (-0.5)).astype(jnp.bfloat16)


def shard_levels(stream_key, shape, split, least, top_value):
    def one(position, parts):
        steps = jax.random.uniform(jax.random.fold_in(jax.random.fold_in(stream_key, 6), position), (parts,), jnp.float32, least / len(split), top_value / len(split))
        return jnp.repeat(jnp.exp(steps), shape[position] // parts).reshape((-1,) + (1,) * (len(shape) - position - 1))

    level = one(*split[0])
    for cut in split[1:]:
        level = level * one(*cut)
    return level


def bell_draw(stream_key, dims, spread, reach, split=(), kind=jnp.bfloat16):
    values = spread * jax.random.normal(stream_key, dims, jnp.float32)
    if split:
        values = values * shard_levels(stream_key, dims, split, -0.22, 0.18)
    return jnp.clip(values, -reach, reach).astype(kind)


def setup_inputs(seed: int = 0) -> dict:
    arg_keys = jax.random.split(jax.random.key(seed), 19)
    tokens = bell_draw(arg_keys[0], (IMAGES, TOK_IMG, D), 1.0, 6.0, ((0, 32),))
    out_grad = bell_draw(arg_keys[1], (IMAGES, TOK_IMG, D), 1.0, 6.0, ((0, 32),))
    image_counts = draw_image_counts(jax.random.fold_in(arg_keys[18], 71), 0)
    table_index = draw_table_index(jax.random.fold_in(arg_keys[18], 71), 0)
    bias_table = draw_bias_table(jax.random.fold_in(arg_keys[18], 71), 0)
    w_input = draw_w_input(jax.random.fold_in(arg_keys[18], 71), 0)
    bias_query = bell_draw(arg_keys[6], (D,), 0.5, 3.0, ((0, 32),))
    bias_value = bell_draw(arg_keys[7], (D,), 0.5, 3.0, ((0, 32),))
    w_output = bell_draw(arg_keys[8], (D, D), (D // 8) ** -0.5, 0.75, ((0, 32),))
    bias_output = bell_draw(arg_keys[9], (D,), 0.5, 3.0, ((0, 32),))
    w_up = bell_draw(arg_keys[10], (D, HID), D ** -0.5, 0.25, ((0, 32),))
    bias_up = bell_draw(arg_keys[11], (HID,), 0.5, 3.0, ((0, 32),))
    w_down = bell_draw(arg_keys[12], (HID, D), (HID // 2) ** -0.5, 0.1875, ((0, 32),))
    bias_down = bell_draw(arg_keys[13], (D,), 0.5, 3.0, ((0, 32),))
    first_gain = jnp.clip(1.0 + 0.1 * jax.random.normal(arg_keys[14], (D,), jnp.float32), 0.5, 1.5).astype(jnp.bfloat16)
    first_shift = bell_draw(arg_keys[15], (D,), 0.3, 2.0, ((0, 32),))
    second_gain = jnp.clip(1.0 + 0.1 * jax.random.normal(arg_keys[16], (D,), jnp.float32), 0.5, 1.5).astype(jnp.bfloat16)
    second_shift = bell_draw(arg_keys[17], (D,), 0.3, 2.0, ((0, 32),))
    return {"tokens": tokens, "out_grad": out_grad, "image_counts": image_counts, "table_index": table_index, "bias_table": bias_table, "w_input": w_input, "bias_query": bias_query, "bias_value": bias_value, "w_output": w_output, "bias_output": bias_output, "w_up": w_up, "bias_up": bias_up, "w_down": w_down, "bias_down": bias_down, "first_gain": first_gain, "first_shift": first_shift, "second_gain": second_gain, "second_shift": second_shift}


EPSILON = 1e-05
ROOT_HALF = 0.7071067811865476
INV_ROOT_TWO_PI = 0.3989422804014327

def rounded(values):
    return lax.optimization_barrier(values.astype(jnp.bfloat16)).astype(jnp.float32)

def layer_norm(values):
    centred = values - lax.optimization_barrier(jnp.mean(values, axis=-1, keepdims=True))
    inverse = lax.rsqrt(lax.optimization_barrier(jnp.mean(centred * centred, axis=-1, keepdims=True)) + EPSILON)
    return (centred * inverse, inverse)

def norm_back(grad_in, normed, inverse, gain):
    scaled = grad_in * gain
    return inverse * (scaled - lax.optimization_barrier(jnp.mean(scaled, axis=-1, keepdims=True)) - normed * lax.optimization_barrier(jnp.mean(scaled * normed, axis=-1, keepdims=True)))

def gelu_value(pre_act):
    return 0.5 * pre_act * (1.0 + jax.scipy.special.erf(pre_act * ROOT_HALF))

def gelu_slope(pre_act):
    return 0.5 * (1.0 + jax.scipy.special.erf(pre_act * ROOT_HALF)) + pre_act * jnp.exp(-0.5 * pre_act * pre_act) * INV_ROOT_TWO_PI

def layer_pass(rows, grad_low, live_rows, params, rel_bias):
    w_input, bias_query, bias_value, w_output, bias_output, w_up, bias_up, w_down, bias_down, first_gain, first_shift, second_gain, second_shift = params
    count = rows.shape[0]
    windows = count // WIN
    scale = HDIM ** (-0.5)

    def split_heads(block):
        return lax.optimization_barrier(block).reshape(windows, WIN, HEADS, HDIM).astype(jnp.float32)
    first_normed, first_inverse = layer_norm(rows)
    first_in = (first_normed * first_gain + first_shift).astype(jnp.bfloat16)
    projected = jnp.dot(first_in, w_input, preferred_element_type=jnp.float32)
    query = ((projected[:, :D] + bias_query) * scale).astype(jnp.bfloat16)
    keys = projected[:, D:2 * D].astype(jnp.bfloat16)
    values = (projected[:, 2 * D:] + bias_value).astype(jnp.bfloat16)
    query_heads = split_heads(query)
    key_heads = split_heads(keys)
    value_heads = split_heads(values)
    scores = jnp.einsum('wqhd,wkhd->whqk', query_heads, key_heads) + rel_bias[None]
    peak = lax.optimization_barrier(jnp.max(scores, axis=-1, keepdims=True))
    log_total = peak + jnp.log(lax.optimization_barrier(jnp.sum(jnp.exp(scores - peak), axis=-1, keepdims=True)))
    attend = jnp.exp(scores - log_total)
    attend_low = rounded(attend)
    head_out = jnp.einsum('whqk,wkhd->wqhd', attend_low, value_heads).reshape(count, D).astype(jnp.bfloat16)
    residual = rows + jnp.dot(head_out, w_output, preferred_element_type=jnp.float32) + bias_output
    second_normed, second_inverse = layer_norm(residual)
    second_in = (second_normed * second_gain + second_shift).astype(jnp.bfloat16)
    pre_act = jnp.dot(second_in, w_up, preferred_element_type=jnp.float32) + bias_up
    activated = gelu_value(pre_act).astype(jnp.bfloat16)
    mixed = ((residual + jnp.dot(activated, w_down, preferred_element_type=jnp.float32) + bias_down) * live_rows).astype(jnp.bfloat16)
    grad_top = grad_low.astype(jnp.float32)
    grad_w_down = jnp.dot(activated.T, grad_low, preferred_element_type=jnp.float32)
    grad_bias_down = lax.optimization_barrier(jnp.sum(grad_top, axis=0))
    grad_pre = jnp.dot(grad_low, w_down.T, preferred_element_type=jnp.float32) * gelu_slope(pre_act)
    grad_pre_low = grad_pre.astype(jnp.bfloat16)
    grad_w_up = jnp.dot(second_in.T, grad_pre_low, preferred_element_type=jnp.float32)
    grad_bias_up = lax.optimization_barrier(jnp.sum(grad_pre, axis=0))
    grad_second = jnp.dot(grad_pre_low, w_up.T, preferred_element_type=jnp.float32)
    grad_second_gain = lax.optimization_barrier(jnp.sum(grad_second * second_normed, axis=0))
    grad_second_shift = lax.optimization_barrier(jnp.sum(grad_second, axis=0))
    grad_residual = grad_top + norm_back(grad_second, second_normed, second_inverse, second_gain)
    grad_res_low = grad_residual.astype(jnp.bfloat16)
    grad_w_output = jnp.dot(head_out.T, grad_res_low, preferred_element_type=jnp.float32)
    grad_bias_output = lax.optimization_barrier(jnp.sum(grad_residual, axis=0))
    grad_heads = split_heads(jnp.dot(grad_res_low, w_output.T, preferred_element_type=jnp.float32).astype(jnp.bfloat16))
    grad_attend = jnp.einsum('wqhd,wkhd->whqk', grad_heads, value_heads)
    grad_value_heads = jnp.einsum('whqk,wqhd->wkhd', attend_low, grad_heads)
    grad_scores = attend * (grad_attend - lax.optimization_barrier(jnp.sum(attend * grad_attend, axis=-1, keepdims=True)))
    grad_bias = lax.optimization_barrier(jnp.sum(grad_scores, axis=0))
    grad_scores_low = rounded(grad_scores)
    grad_query = jnp.einsum('whqk,wkhd->wqhd', grad_scores_low, key_heads).reshape(count, D) * scale
    grad_keys = jnp.einsum('whqk,wqhd->wkhd', grad_scores_low, query_heads).reshape(count, D)
    grad_values = grad_value_heads.reshape(count, D)
    grad_projected = jnp.concatenate([grad_query, grad_keys, grad_values], axis=1).astype(jnp.bfloat16)
    grad_w_input = jnp.dot(first_in.T, grad_projected, preferred_element_type=jnp.float32)
    grad_bias_query = lax.optimization_barrier(jnp.sum(grad_query, axis=0))
    grad_bias_value = lax.optimization_barrier(jnp.sum(grad_values, axis=0))
    grad_first = jnp.dot(grad_projected, w_input.T, preferred_element_type=jnp.float32)
    grad_first_gain = lax.optimization_barrier(jnp.sum(grad_first * first_normed, axis=0))
    grad_first_shift = lax.optimization_barrier(jnp.sum(grad_first, axis=0))
    grad_tokens = grad_residual + norm_back(grad_first, first_normed, first_inverse, first_gain)
    grads = (grad_w_input, grad_bias_query, grad_bias_value, grad_w_output, grad_bias_output, grad_w_up, grad_bias_up, grad_w_down, grad_bias_down, grad_first_gain, grad_first_shift, grad_second_gain, grad_second_shift, grad_bias)
    return (mixed, grad_tokens, grads)

def reference(tokens, out_grad, image_counts, table_index, bias_table, w_input, bias_query, bias_value, w_output, bias_output, w_up, bias_up, w_down, bias_down, first_gain, first_shift, second_gain, second_shift):
    slots = jnp.arange(IMAGES, dtype=jnp.int32)
    live = (slots % IMG_DEV < image_counts[slots // IMG_DEV]).astype(jnp.float32)
    onehot = (table_index.reshape(WIN * WIN)[:, None] == jnp.arange(NREL, dtype=jnp.int32)[None, :]).astype(jnp.float32)
    rel_bias = jnp.dot(onehot, bias_table, precision=lax.Precision.HIGHEST).T.reshape(HEADS, WIN, WIN)
    params = (w_input, bias_query.astype(jnp.float32), bias_value.astype(jnp.float32), w_output, bias_output.astype(jnp.float32), w_up, bias_up.astype(jnp.float32), w_down, bias_down.astype(jnp.float32), first_gain.astype(jnp.float32), first_shift.astype(jnp.float32), second_gain.astype(jnp.float32), second_shift.astype(jnp.float32))
    blocks = IMAGES // 16
    items = (tokens.reshape(blocks, 16 * TOK_IMG, D), out_grad.reshape(blocks, 16 * TOK_IMG, D), live.reshape(blocks, 16))
    start = (jnp.zeros((D, 3 * D), jnp.float32), jnp.zeros((D,), jnp.float32), jnp.zeros((D,), jnp.float32), jnp.zeros((D, D), jnp.float32), jnp.zeros((D,), jnp.float32), jnp.zeros((D, HID), jnp.float32), jnp.zeros((HID,), jnp.float32), jnp.zeros((HID, D), jnp.float32), jnp.zeros((D,), jnp.float32), jnp.zeros((D,), jnp.float32), jnp.zeros((D,), jnp.float32), jnp.zeros((D,), jnp.float32), jnp.zeros((D,), jnp.float32), jnp.zeros((HEADS, WIN, WIN), jnp.float32))

    def advance(carry, item):
        rows_block, grad_block, live_block = item
        live_rows = jnp.repeat(live_block, TOK_IMG)[:, None]
        grad_low = grad_block * live_rows.astype(jnp.bfloat16)
        mixed, grad_tokens, grads = layer_pass(rows_block.astype(jnp.float32), grad_low, live_rows, params, rel_bias)
        return (tuple((a + b for a, b in zip(carry, grads))), (mixed, grad_tokens))
    totals, (mixed, grad_tokens) = lax.scan(advance, start, items)
    grad_table = jnp.dot(onehot.T, totals[13].reshape(HEADS, WIN * WIN).T, precision=lax.Precision.HIGHEST)
    return (mixed.reshape(IMAGES, TOK_IMG, D), grad_tokens.reshape(IMAGES, TOK_IMG, D), totals[0], totals[1], totals[2], totals[3], totals[4], totals[5], totals[6], totals[7], totals[8], totals[9], totals[10], totals[11], totals[12], grad_table)
```

```python
import jax
import jax.numpy as jnp
from jax import lax
from jax.sharding import PartitionSpec as P


HEADS = 16
HDIM = 32
WIN = 49
NREL = 169


EPSILON = 1e-05
ROOT_HALF = 0.7071067811865476
INV_ROOT_TWO_PI = 0.3989422804014327

AXES = ("fsdp", "dp")


def axis_bits(name):
    return (lax.axis_size(name) - 1).bit_length()


def swap(block, name, bit):
    size = lax.axis_size(name)
    return lax.ppermute(block, name, [(i, i ^ (1 << bit)) for i in range(size)])


def routes():
    rest = [("dp", b) for b in range(1, axis_bits("dp"))]
    low = [("fsdp", 0)]
    high = [("fsdp", b) for b in range(1, axis_bits("fsdp"))]
    first = [("dp", 0)]
    return (
        first + rest + low + high,
        first + low + high + rest,
        first + high + rest + low,
    )


def position(name, bit, done):
    dims = [("fsdp", b) for b in reversed(range(axis_bits("fsdp")))]
    dims += [("dp", b) for b in reversed(range(axis_bits("dp")))]
    return [d for d in dims if d not in done].index((name, bit))


def mine_bit(name, bit):
    return (lax.axis_index(name) >> bit) & 1 == 1


def scatter_sum(block, route):
    steps = axis_bits("fsdp") + axis_bits("dp")
    rows = block.shape[0] >> steps
    block = block.reshape((2,) * steps + (rows, block.shape[1]))
    done = []
    for name, bit in route:
        at = position(name, bit, done)
        low = lax.index_in_dim(block, 0, at, keepdims=False)
        high = lax.index_in_dim(block, 1, at, keepdims=False)
        upper = mine_bit(name, bit)
        away = jnp.where(upper, low, high).astype(jnp.bfloat16)
        block = jnp.where(upper, high, low) + swap(away, name, bit).astype(jnp.float32)
        done.append((name, bit))
    return block


def gather_rows(block, route):
    rows, columns = block.shape
    done = list(route)
    for name, bit in reversed(route):
        done.remove((name, bit))
        at = position(name, bit, done)
        other = swap(block, name, bit)
        upper = mine_bit(name, bit)
        block = jnp.stack(
            [jnp.where(upper, other, block), jnp.where(upper, block, other)], axis=at
        )
    return block.reshape(-1, columns)


def gather_split(block):
    ways = routes()
    third = block.shape[1] // 3
    return jnp.concatenate(
        [gather_rows(block[:, i * third : (i + 1) * third], ways[i]) for i in range(3)], axis=1
    )


def sum_all(vector):
    for name, bit in routes()[0]:
        vector = vector + swap(vector, name, bit)
    return vector


def layer_norm(values):
    centred = values - jnp.mean(values, axis=-1, keepdims=True)
    inverse = lax.rsqrt(jnp.mean(centred * centred, axis=-1, keepdims=True) + EPSILON)
    return (centred * inverse, inverse)


def norm_back(grad_in, normed, inverse, gain):
    scaled = grad_in * gain
    return inverse * (
        scaled
        - jnp.mean(scaled, axis=-1, keepdims=True)
        - normed * jnp.mean(scaled * normed, axis=-1, keepdims=True)
    )


def gelu_value(pre_act):
    return 0.5 * pre_act * (1.0 + jax.scipy.special.erf(pre_act * ROOT_HALF))


def gelu_slope(pre_act):
    return (
        0.5 * (1.0 + jax.scipy.special.erf(pre_act * ROOT_HALF))
        + pre_act * jnp.exp(-0.5 * pre_act * pre_act) * INV_ROOT_TWO_PI
    )


def shards(
    tokens,
    out_grad,
    image_counts,
    table_index,
    bias_table,
    w_input,
    bias_query,
    bias_value,
    w_output,
    bias_output,
    w_up,
    bias_up,
    w_down,
    bias_down,
    first_gain,
    first_shift,
    second_gain,
    second_shift,
):
    ways = routes()
    small = (
        bias_query,
        bias_value,
        bias_output,
        bias_up,
        bias_down,
        first_gain,
        first_shift,
        second_gain,
        second_shift,
    )
    small_sizes = [v.shape[0] for v in small]
    small_all = gather_rows(jnp.concatenate(small)[None], ways[0])
    full_small, start = [], 0
    for size in small_sizes:
        full_small.append(small_all[:, start : start + size].reshape(-1))
        start += size
    (
        full_query_bias,
        full_value_bias,
        full_output_bias,
        full_up_bias,
        full_down_bias,
        full_first_gain,
        full_first_shift,
        full_second_gain,
        full_second_shift,
    ) = full_small
    full_input = gather_split(w_input)
    full_output = gather_rows(w_output, ways[0])
    full_up = gather_rows(w_up, ways[1])
    full_down = gather_rows(w_down, ways[2])
    slots = tokens.shape[0]
    tok_image = tokens.shape[1]
    width = tokens.shape[2]
    count = slots * tok_image
    windows = count // WIN
    scale = HDIM ** (-0.5)
    live = (jnp.arange(slots, dtype=jnp.int32) < image_counts[0]).astype(jnp.float32)
    live_rows = jnp.repeat(live, tok_image)[:, None]
    onehot = (
        table_index.reshape(WIN * WIN)[:, None] == jnp.arange(NREL, dtype=jnp.int32)[None, :]
    ).astype(jnp.float32)
    rel_bias = jnp.dot(onehot, bias_table, precision=lax.Precision.HIGHEST).T.reshape(
        HEADS, WIN, WIN
    )
    rows = tokens.reshape(count, width).astype(jnp.float32)
    first_normed, first_inverse = layer_norm(rows)
    first_in = (
        first_normed * full_first_gain.astype(jnp.float32) + full_first_shift.astype(jnp.float32)
    ).astype(jnp.bfloat16)
    projected = jnp.dot(first_in, full_input, preferred_element_type=jnp.float32)
    query = ((projected[:, :width] + full_query_bias.astype(jnp.float32)) * scale).astype(
        jnp.bfloat16
    )
    keys = projected[:, width : 2 * width].astype(jnp.bfloat16)
    values = (projected[:, 2 * width :] + full_value_bias.astype(jnp.float32)).astype(jnp.bfloat16)
    query_heads = query.reshape(windows, WIN, HEADS, HDIM)
    key_heads = keys.reshape(windows, WIN, HEADS, HDIM)
    value_heads = values.reshape(windows, WIN, HEADS, HDIM)
    scores = (
        jnp.einsum("wqhd,wkhd->whqk", query_heads, key_heads, preferred_element_type=jnp.float32)
        + rel_bias[None]
    )
    peak = jnp.max(scores, axis=-1, keepdims=True)
    log_total = peak + jnp.log(jnp.sum(jnp.exp(scores - peak), axis=-1, keepdims=True))
    attend_low = jnp.exp(scores - log_total).astype(jnp.bfloat16)
    head_out = (
        jnp.einsum("whqk,wkhd->wqhd", attend_low, value_heads, preferred_element_type=jnp.float32)
        .reshape(count, width)
        .astype(jnp.bfloat16)
    )
    residual = (
        rows
        + jnp.dot(head_out, full_output, preferred_element_type=jnp.float32)
        + full_output_bias.astype(jnp.float32)
    )
    second_normed, second_inverse = layer_norm(residual)
    second_in = (
        second_normed * full_second_gain.astype(jnp.float32) + full_second_shift.astype(jnp.float32)
    ).astype(jnp.bfloat16)
    pre_act = jnp.dot(second_in, full_up, preferred_element_type=jnp.float32) + full_up_bias.astype(
        jnp.float32
    )
    activated = gelu_value(pre_act).astype(jnp.bfloat16)
    mixed = (
        (
            residual
            + jnp.dot(activated, full_down, preferred_element_type=jnp.float32)
            + full_down_bias.astype(jnp.float32)
        )
        * live_rows
    ).astype(jnp.bfloat16)
    back_input, back_output, back_up, back_down = full_input, full_output, full_up, full_down
    back_first_gain, back_second_gain = full_first_gain, full_second_gain
    grad_low = out_grad.reshape(count, width) * live_rows.astype(jnp.bfloat16)
    grad_top = grad_low.astype(jnp.float32)
    grad_w_down = jnp.dot(activated.T, grad_low, preferred_element_type=jnp.float32)
    grad_bias_down = jnp.sum(grad_top, axis=0)
    grad_pre = jnp.dot(grad_low, back_down.T, preferred_element_type=jnp.float32) * gelu_slope(
        pre_act
    )
    grad_pre_low = grad_pre.astype(jnp.bfloat16)
    grad_w_up = jnp.dot(second_in.T, grad_pre_low, preferred_element_type=jnp.float32)
    grad_bias_up = jnp.sum(grad_pre, axis=0)
    grad_second = jnp.dot(grad_pre_low, back_up.T, preferred_element_type=jnp.float32)
    grad_second_gain = jnp.sum(grad_second * second_normed, axis=0)
    grad_second_shift = jnp.sum(grad_second, axis=0)
    shard_w_down = scatter_sum(grad_w_down, ways[0])
    shard_w_up = scatter_sum(grad_w_up, ways[1])
    grad_residual = grad_top + norm_back(
        grad_second, second_normed, second_inverse, back_second_gain.astype(jnp.float32)
    )
    grad_res_low = grad_residual.astype(jnp.bfloat16)
    grad_w_output = jnp.dot(head_out.T, grad_res_low, preferred_element_type=jnp.float32)
    grad_bias_output = jnp.sum(grad_residual, axis=0)
    grad_heads = (
        jnp.dot(grad_res_low, back_output.T, preferred_element_type=jnp.float32)
        .astype(jnp.bfloat16)
        .reshape(windows, WIN, HEADS, HDIM)
    )
    scores_again = (
        jnp.einsum("wqhd,wkhd->whqk", query_heads, key_heads, preferred_element_type=jnp.float32)
        + rel_bias[None]
    )
    attend = jnp.exp(scores_again - log_total)
    attend_again = attend.astype(jnp.bfloat16)
    grad_attend = jnp.einsum(
        "wqhd,wkhd->whqk", grad_heads, value_heads, preferred_element_type=jnp.float32
    )
    grad_values = jnp.einsum(
        "whqk,wqhd->wkhd", attend_again, grad_heads, preferred_element_type=jnp.float32
    ).reshape(count, width)
    grad_scores = attend * (grad_attend - jnp.sum(attend * grad_attend, axis=-1, keepdims=True))
    grad_bias = jnp.sum(grad_scores, axis=0)
    grad_scores_low = grad_scores.astype(jnp.bfloat16)
    grad_query = (
        jnp.einsum(
            "whqk,wkhd->wqhd", grad_scores_low, key_heads, preferred_element_type=jnp.float32
        ).reshape(count, width)
        * scale
    )
    grad_keys = jnp.einsum(
        "whqk,wqhd->wkhd", grad_scores_low, query_heads, preferred_element_type=jnp.float32
    ).reshape(count, width)
    grad_projected = jnp.concatenate([grad_query, grad_keys, grad_values], axis=1).astype(
        jnp.bfloat16
    )
    grad_w_input = jnp.dot(first_in.T, grad_projected, preferred_element_type=jnp.float32)
    grad_bias_query = jnp.sum(grad_query, axis=0)
    grad_bias_value = jnp.sum(grad_values, axis=0)
    grad_first = jnp.dot(grad_projected, back_input.T, preferred_element_type=jnp.float32)
    grad_first_gain = jnp.sum(grad_first * first_normed, axis=0)
    grad_first_shift = jnp.sum(grad_first, axis=0)
    grad_tokens = grad_residual + norm_back(
        grad_first, first_normed, first_inverse, back_first_gain.astype(jnp.float32)
    )
    third = grad_w_input.shape[1] // 3
    shard_w_input = jnp.concatenate(
        [scatter_sum(grad_w_input[:, i * third : (i + 1) * third], ways[i]) for i in range(3)],
        axis=1,
    )
    shard_w_output = scatter_sum(grad_w_output, ways[2])
    local_table = jnp.dot(
        onehot.T, grad_bias.reshape(HEADS, WIN * WIN).T, precision=lax.Precision.HIGHEST
    )
    vectors = (
        grad_bias_query,
        grad_bias_value,
        grad_bias_output,
        grad_bias_up,
        grad_bias_down,
        grad_first_gain,
        grad_first_shift,
        grad_second_gain,
        grad_second_shift,
    )
    devices = lax.axis_size("fsdp") * lax.axis_size("dp")
    by_device = jnp.concatenate([v.reshape(devices, -1) for v in vectors], axis=1)
    held = by_device.size
    packed = sum_all(jnp.concatenate([by_device.reshape(-1), local_table.reshape(-1)]))
    grad_table = packed[held:].reshape(local_table.shape)
    own = lax.dynamic_index_in_dim(
        packed[:held].reshape(by_device.shape), lax.axis_index(AXES), 0, keepdims=False
    )
    shards_small, start = [], 0
    for size in small_sizes:
        shards_small.append(own[start : start + size])
        start += size
    (
        shard_bias_query,
        shard_bias_value,
        shard_bias_output,
        shard_bias_up,
        shard_bias_down,
        shard_first_gain,
        shard_first_shift,
        shard_second_gain,
        shard_second_shift,
    ) = shards_small
    return (
        mixed.reshape(slots, tok_image, width),
        grad_tokens.reshape(slots, tok_image, width),
        shard_w_input,
        shard_bias_query,
        shard_bias_value,
        shard_w_output,
        shard_bias_output,
        shard_w_up,
        shard_bias_up,
        shard_w_down,
        shard_bias_down,
        shard_first_gain,
        shard_first_shift,
        shard_second_gain,
        shard_second_shift,
        grad_table,
    )


def solution(mesh):
    return jax.shard_map(
        shards,
        mesh=mesh,
        in_specs=(
            P(("fsdp", "dp"), None, None),
            P(("fsdp", "dp"), None, None),
            P(("fsdp", "dp")),
            P(),
            P(),
            P(("fsdp", "dp"), None),
            P(("fsdp", "dp")),
            P(("fsdp", "dp")),
            P(("fsdp", "dp"), None),
            P(("fsdp", "dp")),
            P(("fsdp", "dp"), None),
            P(("fsdp", "dp")),
            P(("fsdp", "dp"), None),
            P(("fsdp", "dp")),
            P(("fsdp", "dp")),
            P(("fsdp", "dp")),
            P(("fsdp", "dp")),
            P(("fsdp", "dp")),
        ),
        out_specs=(
            P(("fsdp", "dp"), None, None),
            P(("fsdp", "dp"), None, None),
            P(("fsdp", "dp"), None),
            P(("fsdp", "dp")),
            P(("fsdp", "dp")),
            P(("fsdp", "dp"), None),
            P(("fsdp", "dp")),
            P(("fsdp", "dp"), None),
            P(("fsdp", "dp")),
            P(("fsdp", "dp"), None),
            P(("fsdp", "dp")),
            P(("fsdp", "dp")),
            P(("fsdp", "dp")),
            P(("fsdp", "dp")),
            P(("fsdp", "dp")),
            P(),
        ),
        check_vma=False,
    )
```

```python
import jax
import jax.numpy as jnp
from jax import lax
from jax.sharding import PartitionSpec as P


HEADS = 16
HDIM = 32
WIN = 49
NREL = 169


EPSILON = 1e-05
ROOT_HALF = 0.7071067811865476
INV_ROOT_TWO_PI = 0.3989422804014327

AXES = ("fsdp", "dp")


def axis_bits(name):
    return (lax.axis_size(name) - 1).bit_length()


def swap(block, name, bit):
    size = lax.axis_size(name)
    return lax.ppermute(block, name, [(i, i ^ (1 << bit)) for i in range(size)])


def routes():
    rest = [("dp", b) for b in range(1, axis_bits("dp"))]
    low = [("fsdp", 0)]
    high = [("fsdp", b) for b in range(1, axis_bits("fsdp"))]
    first = [("dp", 0)]
    return (
        first + rest + low + high,
        first + low + high + rest,
        first + high + rest + low,
    )


def position(name, bit, done):
    dims = [("fsdp", b) for b in reversed(range(axis_bits("fsdp")))]
    dims += [("dp", b) for b in reversed(range(axis_bits("dp")))]
    return [d for d in dims if d not in done].index((name, bit))


def mine_bit(name, bit):
    return (lax.axis_index(name) >> bit) & 1 == 1


def scatter_sum(block, route):
    steps = axis_bits("fsdp") + axis_bits("dp")
    rows = block.shape[0] >> steps
    block = block.reshape((2,) * steps + (rows, block.shape[1]))
    done = []
    for name, bit in route:
        at = position(name, bit, done)
        low = lax.index_in_dim(block, 0, at, keepdims=False)
        high = lax.index_in_dim(block, 1, at, keepdims=False)
        upper = mine_bit(name, bit)
        away = jnp.where(upper, low, high).astype(jnp.bfloat16)
        block = jnp.where(upper, high, low) + swap(away, name, bit).astype(jnp.float32)
        done.append((name, bit))
    return block


def gather_rows(block, route):
    rows, columns = block.shape
    done = list(route)
    for name, bit in reversed(route):
        done.remove((name, bit))
        at = position(name, bit, done)
        other = swap(block, name, bit)
        upper = mine_bit(name, bit)
        block = jnp.stack(
            [jnp.where(upper, other, block), jnp.where(upper, block, other)], axis=at
        )
    return block.reshape(-1, columns)


def sum_all(vector):
    for name, bit in routes()[0]:
        vector = vector + swap(vector, name, bit)
    return vector


def layer_norm(values):
    centred = values - jnp.mean(values, axis=-1, keepdims=True)
    inverse = lax.rsqrt(jnp.mean(centred * centred, axis=-1, keepdims=True) + EPSILON)
    return (centred * inverse, inverse)


def norm_back(grad_in, normed, inverse, gain):
    scaled = grad_in * gain
    return inverse * (
        scaled
        - jnp.mean(scaled, axis=-1, keepdims=True)
        - normed * jnp.mean(scaled * normed, axis=-1, keepdims=True)
    )


def gelu_value(pre_act):
    return 0.5 * pre_act * (1.0 + jax.scipy.special.erf(pre_act * ROOT_HALF))


def gelu_slope(pre_act):
    return (
        0.5 * (1.0 + jax.scipy.special.erf(pre_act * ROOT_HALF))
        + pre_act * jnp.exp(-0.5 * pre_act * pre_act) * INV_ROOT_TWO_PI
    )


def shards(
    tokens,
    out_grad,
    image_counts,
    table_index,
    bias_table,
    w_input,
    bias_query,
    bias_value,
    w_output,
    bias_output,
    w_up,
    bias_up,
    w_down,
    bias_down,
    first_gain,
    first_shift,
    second_gain,
    second_shift,
):
    ways = routes()
    small = (
        bias_query,
        bias_value,
        bias_output,
        bias_up,
        bias_down,
        first_gain,
        first_shift,
        second_gain,
        second_shift,
    )
    small_sizes = [v.shape[0] for v in small]
    holders = lax.axis_size("fsdp") * lax.axis_size("dp")
    packed_small = jnp.concatenate(small).reshape(w_input.shape[0], -1)
    half = (w_input.shape[1] + w_output.shape[1]) // 2
    left = gather_rows(jnp.concatenate([w_input[:, :half], packed_small], axis=1), ways[0])
    right = gather_rows(jnp.concatenate([w_input[:, half:], w_output], axis=1), ways[1])
    full_input = jnp.concatenate([left[:, :half], right[:, : w_input.shape[1] - half]], axis=1)
    full_output = right[:, w_input.shape[1] - half :]
    small_all = left[:, half:].reshape(holders, -1)
    full_small, start = [], 0
    for size in small_sizes:
        full_small.append(small_all[:, start : start + size].reshape(-1))
        start += size
    (
        full_query_bias,
        full_value_bias,
        full_output_bias,
        full_up_bias,
        full_down_bias,
        full_first_gain,
        full_first_shift,
        full_second_gain,
        full_second_shift,
    ) = full_small
    full_up = gather_rows(w_up, ways[1])
    full_down = gather_rows(w_down, ways[2])
    slots = tokens.shape[0]
    tok_image = tokens.shape[1]
    width = tokens.shape[2]
    count = slots * tok_image
    windows = count // WIN
    scale = HDIM ** (-0.5)
    live = (jnp.arange(slots, dtype=jnp.int32) < image_counts[0]).astype(jnp.float32)
    live_rows = jnp.repeat(live, tok_image)[:, None]
    onehot = (
        table_index.reshape(WIN * WIN)[:, None] == jnp.arange(NREL, dtype=jnp.int32)[None, :]
    ).astype(jnp.float32)
    rel_bias = jnp.dot(onehot, bias_table, precision=lax.Precision.HIGHEST).T.reshape(
        HEADS, WIN, WIN
    )
    rows = tokens.reshape(count, width).astype(jnp.float32)
    first_normed, first_inverse = layer_norm(rows)
    first_in = (
        first_normed * full_first_gain.astype(jnp.float32) + full_first_shift.astype(jnp.float32)
    ).astype(jnp.bfloat16)
    projected = jnp.dot(first_in, full_input, preferred_element_type=jnp.float32)
    query = ((projected[:, :width] + full_query_bias.astype(jnp.float32)) * scale).astype(
        jnp.bfloat16
    )
    keys = projected[:, width : 2 * width].astype(jnp.bfloat16)
    values = (projected[:, 2 * width :] + full_value_bias.astype(jnp.float32)).astype(jnp.bfloat16)
    query_heads = query.reshape(windows, WIN, HEADS, HDIM)
    key_heads = keys.reshape(windows, WIN, HEADS, HDIM)
    value_heads = values.reshape(windows, WIN, HEADS, HDIM)
    scores = (
        jnp.einsum("wqhd,wkhd->whqk", query_heads, key_heads, preferred_element_type=jnp.float32)
        + rel_bias[None]
    )
    peak = jnp.max(scores, axis=-1, keepdims=True)
    log_total = peak + jnp.log(jnp.sum(jnp.exp(scores - peak), axis=-1, keepdims=True))
    attend_low = jnp.exp(scores - log_total).astype(jnp.bfloat16)
    head_out = (
        jnp.einsum("whqk,wkhd->wqhd", attend_low, value_heads, preferred_element_type=jnp.float32)
        .reshape(count, width)
        .astype(jnp.bfloat16)
    )
    residual = (
        rows
        + jnp.dot(head_out, full_output, preferred_element_type=jnp.float32)
        + full_output_bias.astype(jnp.float32)
    )
    second_normed, second_inverse = layer_norm(residual)
    second_in = (
        second_normed * full_second_gain.astype(jnp.float32) + full_second_shift.astype(jnp.float32)
    ).astype(jnp.bfloat16)
    pre_act = jnp.dot(second_in, full_up, preferred_element_type=jnp.float32) + full_up_bias.astype(
        jnp.float32
    )
    activated = gelu_value(pre_act).astype(jnp.bfloat16)
    mixed = (
        (
            residual
            + jnp.dot(activated, full_down, preferred_element_type=jnp.float32)
            + full_down_bias.astype(jnp.float32)
        )
        * live_rows
    ).astype(jnp.bfloat16)
    back_input, back_output, back_up, back_down = full_input, full_output, full_up, full_down
    back_first_gain, back_second_gain = full_first_gain, full_second_gain
    grad_low = out_grad.reshape(count, width) * live_rows.astype(jnp.bfloat16)
    grad_top = grad_low.astype(jnp.float32)
    grad_w_down = jnp.dot(activated.T, grad_low, preferred_element_type=jnp.float32)
    grad_bias_down = jnp.sum(grad_top, axis=0)
    grad_pre = jnp.dot(grad_low, back_down.T, preferred_element_type=jnp.float32) * gelu_slope(
        pre_act
    )
    grad_pre_low = grad_pre.astype(jnp.bfloat16)
    grad_w_up = jnp.dot(second_in.T, grad_pre_low, preferred_element_type=jnp.float32)
    grad_bias_up = jnp.sum(grad_pre, axis=0)
    grad_second = jnp.dot(grad_pre_low, back_up.T, preferred_element_type=jnp.float32)
    grad_second_gain = jnp.sum(grad_second * second_normed, axis=0)
    grad_second_shift = jnp.sum(grad_second, axis=0)
    shard_w_down = scatter_sum(grad_w_down, ways[0])
    shard_w_up = scatter_sum(grad_w_up, ways[1])
    grad_residual = grad_top + norm_back(
        grad_second, second_normed, second_inverse, back_second_gain.astype(jnp.float32)
    )
    grad_res_low = grad_residual.astype(jnp.bfloat16)
    grad_w_output = jnp.dot(head_out.T, grad_res_low, preferred_element_type=jnp.float32)
    grad_bias_output = jnp.sum(grad_residual, axis=0)
    grad_heads = (
        jnp.dot(grad_res_low, back_output.T, preferred_element_type=jnp.float32)
        .astype(jnp.bfloat16)
        .reshape(windows, WIN, HEADS, HDIM)
    )
    scores_again = (
        jnp.einsum("wqhd,wkhd->whqk", query_heads, key_heads, preferred_element_type=jnp.float32)
        + rel_bias[None]
    )
    attend = jnp.exp(scores_again - log_total)
    attend_again = attend.astype(jnp.bfloat16)
    grad_attend = jnp.einsum(
        "wqhd,wkhd->whqk", grad_heads, value_heads, preferred_element_type=jnp.float32
    )
    grad_values = jnp.einsum(
        "whqk,wqhd->wkhd", attend_again, grad_heads, preferred_element_type=jnp.float32
    ).reshape(count, width)
    grad_scores = attend * (grad_attend - jnp.sum(attend * grad_attend, axis=-1, keepdims=True))
    grad_bias = jnp.sum(grad_scores, axis=0)
    grad_scores_low = grad_scores.astype(jnp.bfloat16)
    grad_query = (
        jnp.einsum(
            "whqk,wkhd->wqhd", grad_scores_low, key_heads, preferred_element_type=jnp.float32
        ).reshape(count, width)
        * scale
    )
    grad_keys = jnp.einsum(
        "whqk,wqhd->wkhd", grad_scores_low, query_heads, preferred_element_type=jnp.float32
    ).reshape(count, width)
    grad_projected = jnp.concatenate([grad_query, grad_keys, grad_values], axis=1).astype(
        jnp.bfloat16
    )
    grad_w_input = jnp.dot(first_in.T, grad_projected, preferred_element_type=jnp.float32)
    grad_bias_query = jnp.sum(grad_query, axis=0)
    grad_bias_value = jnp.sum(grad_values, axis=0)
    grad_first = jnp.dot(grad_projected, back_input.T, preferred_element_type=jnp.float32)
    grad_first_gain = jnp.sum(grad_first * first_normed, axis=0)
    grad_first_shift = jnp.sum(grad_first, axis=0)
    grad_tokens = grad_residual + norm_back(
        grad_first, first_normed, first_inverse, back_first_gain.astype(jnp.float32)
    )
    sum_left = scatter_sum(grad_w_input[:, :half], ways[0])
    sum_right = scatter_sum(
        jnp.concatenate([grad_w_input[:, half:], grad_w_output], axis=1), ways[1]
    )
    rest = grad_w_input.shape[1] - half
    shard_w_input = jnp.concatenate([sum_left, sum_right[:, :rest]], axis=1)
    shard_w_output = sum_right[:, rest:]
    local_table = jnp.dot(
        onehot.T, grad_bias.reshape(HEADS, WIN * WIN).T, precision=lax.Precision.HIGHEST
    )
    vectors = (
        grad_bias_query,
        grad_bias_value,
        grad_bias_output,
        grad_bias_up,
        grad_bias_down,
        grad_first_gain,
        grad_first_shift,
        grad_second_gain,
        grad_second_shift,
    )
    devices = lax.axis_size("fsdp") * lax.axis_size("dp")
    by_device = jnp.concatenate([v.reshape(devices, -1) for v in vectors], axis=1)
    held = by_device.size
    packed = sum_all(jnp.concatenate([by_device.reshape(-1), local_table.reshape(-1)]))
    grad_table = packed[held:].reshape(local_table.shape)
    own = lax.dynamic_index_in_dim(
        packed[:held].reshape(by_device.shape), lax.axis_index(AXES), 0, keepdims=False
    )
    shards_small, start = [], 0
    for size in small_sizes:
        shards_small.append(own[start : start + size])
        start += size
    (
        shard_bias_query,
        shard_bias_value,
        shard_bias_output,
        shard_bias_up,
        shard_bias_down,
        shard_first_gain,
        shard_first_shift,
        shard_second_gain,
        shard_second_shift,
    ) = shards_small
    return (
        mixed.reshape(slots, tok_image, width),
        grad_tokens.reshape(slots, tok_image, width),
        shard_w_input,
        shard_bias_query,
        shard_bias_value,
        shard_w_output,
        shard_bias_output,
        shard_w_up,
        shard_bias_up,
        shard_w_down,
        shard_bias_down,
        shard_first_gain,
        shard_first_shift,
        shard_second_gain,
        shard_second_shift,
        grad_table,
    )


def solution(mesh):
    return jax.shard_map(
        shards,
        mesh=mesh,
        in_specs=(
            P(("fsdp", "dp"), None, None),
            P(("fsdp", "dp"), None, None),
            P(("fsdp", "dp")),
            P(),
            P(),
            P(("fsdp", "dp"), None),
            P(("fsdp", "dp")),
            P(("fsdp", "dp")),
            P(("fsdp", "dp"), None),
            P(("fsdp", "dp")),
            P(("fsdp", "dp"), None),
            P(("fsdp", "dp")),
            P(("fsdp", "dp"), None),
            P(("fsdp", "dp")),
            P(("fsdp", "dp")),
            P(("fsdp", "dp")),
            P(("fsdp", "dp")),
            P(("fsdp", "dp")),
        ),
        out_specs=(
            P(("fsdp", "dp"), None, None),
            P(("fsdp", "dp"), None, None),
            P(("fsdp", "dp"), None),
            P(("fsdp", "dp")),
            P(("fsdp", "dp")),
            P(("fsdp", "dp"), None),
            P(("fsdp", "dp")),
            P(("fsdp", "dp"), None),
            P(("fsdp", "dp")),
            P(("fsdp", "dp"), None),
            P(("fsdp", "dp")),
            P(("fsdp", "dp")),
            P(("fsdp", "dp")),
            P(("fsdp", "dp")),
            P(("fsdp", "dp")),
            P(),
        ),
        check_vma=False,
    )
```
